32 devices in a mesh: seq: 4 (over z), head: 8 (over y, x, core).
Axes of the slice: x: 2, y: 2, z: 4, core: 2. Of those that a mesh axis runs over, the one named last changes fastest.
Arguments:
- queries: bfloat16 [4096, 2048], P(('seq', 'head')), may hold values from -6 to 6
- key_rows: bfloat16 [4096, 2048], P(('seq', 'head')), may hold values from -6 to 6
- value_rows: bfloat16 [4096, 2048], P(('seq', 'head')), may hold values from -6 to 6
- ridge_diag: float32 [16, 128], replicated, may hold values from 0.5 to 4
Outputs:
- mixed: bfloat16 [4096, 2048], P(('seq', 'head'))
The draws below stay inside these ranges and needn't reach their ends.
All inputs are finite; a program needn't handle non-finite values.
Results may differ from the reference program's by a relative error of at most 0.0075.
The reference program's roundings to bfloat16 on the way (of `q_unit` and `k_unit`) count: a program that leaves them out, or rounds other values in their place, can miss the bound.
Values may be sent and summed in bfloat16 or wider, within the bound.
A program may use at most 64 MiB of HBM per device.

```python
import math
import jax
import jax.numpy as jnp
from jax import lax

HEADS = 16
DK = 128
GROUP = 64
TOK_DEV = 128
TOKENS = 4096


def draw_key_rows(key, part):
    rank_count = max(DK // 8, 2)
    switch_len = 16 * GROUP
    segment_count = TOKENS // switch_len + 2
    shift_key = jax.random.fold_in(key, 11)
    basis_key = jax.random.fold_in(key, 12)
    coeff_key = jax.random.fold_in(key, 13)
    noise_key = jax.random.fold_in(key, 14)
    shift_by = jax.random.randint(shift_key, (HEADS,), 0, switch_len, dtype=jnp.int32)
    positions = jnp.arange(TOKENS, dtype=jnp.int32)
    segment = (positions[:, None] + shift_by[None, :]) // switch_len
    basis = jax.random.normal(basis_key, (rank_count, HEADS, segment_count, DK), jnp.float32)
    coeffs = jax.random.normal(coeff_key, (TOKENS, HEADS, rank_count), jnp.float32)
    noise = 0.05 * jax.random.normal(noise_key, (TOKENS, HEADS, DK), jnp.float32)
    grade = jnp.exp(-jnp.log(10.0) * jnp.arange(rank_count, dtype=jnp.float32) / (rank_count - 1))
    head_index = jnp.arange(HEADS, dtype=jnp.int32)[None, :]
    total = noise
    for which in range(rank_count):
        picked = basis[which][head_index, segment]
        total = total + (coeffs[:, :, which] * grade[which])[:, :, None] * picked
    return jnp.clip(total, -6.0, 6.0).reshape(TOKENS, HEADS * DK).astype(jnp.bfloat16)


def shard_levels(own_key, extent, pieces, low, largest):
    factor_of, own = 1.0, jax.random.fold_in(own_key, 6)
    for dim, parts in pieces:
        steps = jnp.exp(jax.random.uniform(jax.random.fold_in(own, dim), (parts,), jnp.float32, low / len(pieces), largest / len(pieces)))
        factor_of = factor_of * jnp.repeat(steps, extent[dim] // parts).reshape([-1 if axis == dim else 1 for axis in range(len(extent))])
    return factor_of


def gaussian(key, shape, deviation, most, cuts=(), kind=jnp.bfloat16):
    entries = deviation * jax.random.normal(key, shape, jnp.float32)
    if cuts:
        entries = entries * shard_levels(key, shape, cuts, -0.22, 0.18)
    return jnp.clip(entries, -most, most).astype(kind)


def setup_inputs(seed: int = 0) -> dict:
    seeds = jax.random.split(jax.random.key(seed), 5)
    queries = gaussian(seeds[0], (TOKENS, HEADS * DK), 1.0, 6.0, ((0, 32),))
    key_rows = draw_key_rows(jax.random.fold_in(seeds[4], 71), 0)
    value_rows = gaussian(seeds[2], (TOKENS, HEADS * DK), 1.0, 6.0, ((0, 32),))
    ridge_diag = jnp.clip(jnp.exp(jax.random.uniform(seeds[3], (HEADS, DK), jnp.float32, math.log(0.5), math.log(4.0))), 0.5, 4.0)
    return dict(queries=queries, key_rows=key_rows, value_rows=value_rows, ridge_diag=ridge_diag)


epsilon = 1e-06
highest = lax.Precision.HIGHEST

def unit_rows(matrix):
    values_f = matrix.astype(jnp.float32)
    scale_back = lax.rsqrt(lax.optimization_barrier(jnp.sum(values_f * values_f, axis=-1, keepdims=True)) + epsilon)
    return (values_f * scale_back).astype(jnp.bfloat16)

def reference(queries, key_rows, value_rows, ridge_diag):
    per_block = TOK_DEV // GROUP
    block_count = TOKENS // TOK_DEV

    def head_out(head_index):
        offset = head_index * DK
        q_head = lax.dynamic_slice_in_dim(queries, offset, DK, 1)
        k_head = lax.dynamic_slice_in_dim(key_rows, offset, DK, 1)
        v_head = lax.dynamic_slice_in_dim(value_rows, offset, DK, 1)
        ridge_here = lax.dynamic_slice_in_dim(ridge_diag, head_index, 1, 0)[0]
        q_unit = unit_rows(q_head).reshape(block_count, per_block, GROUP, DK)
        k_unit = unit_rows(k_head).reshape(block_count, per_block, GROUP, DK)
        v_block = v_head.reshape(block_count, per_block, GROUP, DK)

        def advance(running, inputs_now):
            gram_run, vk_run = running
            q_now, k_now, v_now = inputs_now
            k_f = k_now.astype(jnp.float32)
            v_f = v_now.astype(jnp.float32)
            group_gram = jnp.einsum('cti,ctj->cij', k_f, k_f, precision=highest)
            group_vk = jnp.einsum('ctv,ctk->cvk', v_f, k_f, precision=highest)
            gram_inc = jnp.cumsum(group_gram, axis=0)
            vk_inc = jnp.cumsum(group_vk, axis=0)
            gram_start = gram_run + gram_inc - group_gram
            vk_start = vk_run + vk_inc - group_vk
            system = gram_start + jnp.diag(ridge_here)
            factor = jnp.linalg.cholesky(system)
            targets = jnp.swapaxes(q_now.astype(jnp.float32), -1, -2)
            half_solved = jax.scipy.linalg.solve_triangular(factor, targets, lower=True)
            solved = jax.scipy.linalg.solve_triangular(factor, half_solved, lower=True, trans=1)
            carried = jnp.einsum('cvk,ckt->ctv', vk_start, solved, precision=highest)
            scores = jnp.einsum('csk,ckt->cts', k_f, solved, precision=highest)
            causal = jnp.arange(GROUP)[None, :] <= jnp.arange(GROUP)[:, None]
            within = jnp.einsum('cts,csv->ctv', jnp.where(causal[None], scores, 0.0), v_f, precision=highest)
            result = (carried + within).astype(jnp.bfloat16)
            return ((gram_run + gram_inc[-1], vk_run + vk_inc[-1]), result)
        zero_state = jnp.zeros((DK, DK), jnp.float32)
        _, outputs = lax.scan(advance, (zero_state, zero_state), (q_unit, k_unit, v_block))
        return outputs.reshape(TOKENS, DK)
    stacked = lax.map(head_out, jnp.arange(HEADS, dtype=jnp.int32))
    return jnp.transpose(stacked, (1, 0, 2)).reshape(TOKENS, HEADS * DK)
```

```python
import functools

import jax
import jax.numpy as jnp
from jax import lax
from jax.experimental import pallas as pl
from jax.experimental.pallas import tpu as pltpu
from jax.sharding import PartitionSpec as P

DK = 128
GROUP = 64
EDGE = 32
PACK = DK // EDGE
STEP_PACKS = 4
CHUNK = 64
EPS = 1e-06
F32 = jnp.float32
BF16 = jnp.bfloat16


def unit(rows):
    wide = rows.astype(F32)
    back = lax.rsqrt(jnp.sum(wide * wide, axis=-1, keepdims=True) + EPS)
    return (wide * back).astype(BF16)


def split3(value):
    high = value.astype(BF16)
    rest = value - high.astype(F32)
    mid = rest.astype(BF16)
    low = (rest - mid.astype(F32)).astype(BF16)
    return high, mid, low


def dot(left, right, contract):
    return lax.dot_general(left, right, ((contract[:1], contract[1:]), ((), ())), preferred_element_type=F32)


def left_stack(parts):
    high, mid, low = parts
    return jnp.concatenate([high, high, mid, high, low, mid], axis=0)


def right_stack(parts):
    high, mid, low = parts
    return jnp.concatenate([high, mid, high, low, high, mid], axis=0)


def sweep_round(rows, lane, sub, turn):
    base = (lane // EDGE) * EDGE
    within = lane - base

    def take(block, pick):
        return jnp.take_along_axis(block, pick, axis=1, mode="promise_in_bounds")

    j = turn
    at, inner = j // 8, j % 8
    first, second = within == j, within == j + 1
    either = jnp.logical_or(first, second)
    pick1, pick2 = base + j, base + j + 1
    row1 = jnp.broadcast_to(rows[at][inner : inner + 1, :], rows[at].shape)
    row2 = jnp.broadcast_to(rows[at][inner + 1 : inner + 2, :], rows[at].shape)
    a, b, d = take(row1, pick1), take(row1, pick2), take(row2, pick2)
    inv1 = 1.0 / a
    ratio = b * inv1
    inv2 = 1.0 / (d - b * ratio)
    scaled1 = jnp.where(first, -1.0, row1) * inv1
    scaled2 = jnp.where(second, -1.0, jnp.where(first, 0.0, row2) - b * scaled1) * inv2
    scaled1 = jnp.where(second, 0.0, scaled1)
    fresh = []
    for v, block in enumerate(rows):
        col1, col2 = take(block, pick1), take(block, pick2)
        gone = either
        if v == at:
            here1, here2 = sub == inner, sub == inner + 1
            col1 = jnp.where(here1, -1.0, col1)
            col2 = jnp.where(here2, -1.0, jnp.where(here1, 0.0, col2) - col1 * ratio)
            col1 = jnp.where(here2, 0.0, col1)
            gone = jnp.logical_or(either, jnp.logical_or(here1, here2))
        else:
            col2 = col2 - col1 * ratio
        fresh.append(jnp.where(gone, 0.0, block) - col1 * scaled1 - col2 * scaled2)
    return fresh


def invert_all(sys_ref, pinv_ref, midway):
    count = sys_ref.shape[0]
    packs = count // PACK
    lane = lax.broadcasted_iota(jnp.int32, (8, DK), 1)
    sub = lax.broadcasted_iota(jnp.int32, (8, DK), 0)
    lane32 = lax.broadcasted_iota(jnp.int32, (EDGE, DK), 1)
    sub32 = lax.broadcasted_iota(jnp.int32, (EDGE, DK), 0)
    row128 = lax.broadcasted_iota(jnp.int32, (DK, DK), 0) // EDGE
    lane128 = lax.broadcasted_iota(jnp.int32, (DK, DK), 1) // EDGE

    def panel(p, carry):
        @pl.when(p == PACK // 2)
        def _():
            midway()

        start = pl.multiple_of(p * EDGE, EDGE)
        all_rows = []
        for g in range(packs):
            packed = None
            for k in range(PACK):
                piece = sys_ref[g * PACK + k, pl.ds(start, EDGE), :]
                piece = pltpu.roll(piece, lax.rem((k - p) * EDGE + DK, DK), 1)
                packed = piece if packed is None else jnp.where(lane32 // EDGE == k, piece, packed)
            all_rows.append([packed[8 * v : 8 * v + 8, :] for v in range(EDGE // 8)])
        for turn in range(0, EDGE, 2):
            all_rows = [sweep_round(rows, lane, sub, turn) for rows in all_rows]
        for g in range(packs):
            pinv_ref[g] = jnp.concatenate(all_rows[g], axis=0)

        mine = lane32 // EDGE == p
        diag = lane32 - p * EDGE == sub32
        cleared = jnp.logical_or(row128 == p, lane128 == p)

        def update(turn, carry):
            batch = [turn * STEP_PACKS + i for i in range(STEP_PACKS)]
            rows, inverses = [], []
            for g in batch:
                inverses.append(jnp.transpose(left_stack(split3(pinv_ref[g]))))
                for k in range(PACK):
                    rows.append(sys_ref[g * PACK + k, pl.ds(start, EDGE), :])
            rows = [split3(jnp.where(mine, jnp.where(diag, -1.0, 0.0), r)) for r in rows]
            scaled = []
            for i in range(STEP_PACKS):
                for k in range(PACK):
                    left = inverses[i][k * EDGE : (k + 1) * EDGE, :]
                    scaled.append(dot(left, right_stack(rows[i * PACK + k]), (1, 0)))
            change = [dot(left_stack(r), right_stack(split3(t)), (0, 0)) for r, t in zip(rows, scaled)]
            for i, c in enumerate(change):
                s = turn * STEP_PACKS * PACK + i
                sys_ref[s] = jnp.where(cleared, 0.0, sys_ref[s]) + c
            return carry

        return lax.fori_loop(0, packs // STEP_PACKS, update, carry)

    lax.fori_loop(0, PACK, panel, 0)


def whole_kernel(
    owners, shards, q_hbm, k_hbm, v_hbm, ridge_ref, out_hbm,
    q_all, k_all, v_all, sys_ref, vk_ref, pinv_ref, stage, gram_total, vk_total, gram_staged, vk_staged, gram_before, vk_before,
    send_sems, recv_sems, local_sems, out_send, out_recv, out_local, gram_send, gram_recv, vk_send, vk_recv,
):
    me, shard = lax.axis_index("head"), lax.axis_index("seq")
    rows_each = q_hbm.shape[0]
    width = q_all.shape[1]
    heads = width // DK
    per_source = rows_each // GROUP
    groups = owners * per_source
    moved = ((k_hbm, k_all), (v_hbm, v_all), (q_hbm, q_all))

    def rows_of(source):
        return pl.ds(pl.multiple_of(source * rows_each, rows_each), rows_each)

    def cols_of(owner):
        return pl.ds(pl.multiple_of(owner * width, width), width)

    def incoming(kind, source):
        return pltpu.make_async_remote_copy(
            src_ref=moved[kind][0].at[:, cols_of(source)],
            dst_ref=moved[kind][1].at[rows_of(source), :],
            send_sem=send_sems.at[kind, source],
            recv_sem=recv_sems.at[kind, source],
            device_id={"head": source},
            device_id_type=pl.DeviceIdType.MESH,
        )

    def outgoing(kind, peer):
        return pltpu.make_async_remote_copy(
            src_ref=moved[kind][0].at[:, cols_of(peer)],
            dst_ref=moved[kind][1].at[rows_of(me), :],
            send_sem=send_sems.at[kind, peer],
            recv_sem=recv_sems.at[kind, me],
            device_id={"head": peer},
            device_id_type=pl.DeviceIdType.MESH,
        )

    def own(kind):
        return pltpu.make_async_copy(
            moved[kind][0].at[:, cols_of(me)], moved[kind][1].at[rows_of(me), :], local_sems.at[kind]
        )

    def chunk(c):
        return c * CHUNK // DK, pl.ds(c * CHUNK % DK, CHUNK)

    def link_copy(staged, before, send, recv, c, target):
        head, rows = chunk(c)
        return pltpu.make_async_remote_copy(
            src_ref=staged.at[head, rows, :],
            dst_ref=before.at[head, rows, :],
            send_sem=send.at[c],
            recv_sem=recv.at[c],
            device_id={"seq": target},
            device_id_type=pl.DeviceIdType.MESH,
        )

    chunks = heads * DK // CHUNK

    def chain(total, staged, before, send, recv):
        for c in range(chunks):
            head, rows = chunk(c)

            @pl.when(shard > 0)
            def _():
                link_copy(staged, before, send, recv, c, shard).wait_recv()

            @pl.when(shard + 1 < shards)
            def _():
                staged[head, rows, :] = total[head, rows, :] + before[head, rows, :]
                link_copy(staged, before, send, recv, c, shard + 1).start()

    def drain(staged, before, send, recv):
        for c in range(chunks):
            @pl.when(shard + 1 < shards)
            def _():
                link_copy(staged, before, send, recv, c, shard + 1).wait_send()

    barrier = pltpu.get_barrier_semaphore()
    for step in range(1, owners):
        pl.semaphore_signal(barrier, inc=1, device_id={"head": lax.rem(me + step, owners)}, device_id_type=pl.DeviceIdType.MESH)
    for near in (shard - 1, shard + 1):
        @pl.when(jnp.logical_and(near >= 0, near < shards))
        def _():
            pl.semaphore_signal(barrier, inc=1, device_id={"seq": near}, device_id_type=pl.DeviceIdType.MESH)
    for kind in range(3):
        own(kind).start()
    ends = (shard == 0).astype(jnp.int32) + (shard == shards - 1).astype(jnp.int32)
    pl.semaphore_wait(barrier, owners - 1 + 2 - ends)
    for kind in range(3):
        for step in range(1, owners):
            outgoing(kind, lax.rem(me + step, owners)).start()
    for kind in range(3):
        own(kind).wait()

    @pl.when(shard == 0)
    def _():
        gram_before[...] = jnp.zeros_like(gram_before)
        vk_before[...] = jnp.zeros_like(vk_before)

    def rows_in(source, i):
        return pl.ds(pl.multiple_of(source * rows_each + i * GROUP, GROUP), GROUP)

    def keys_in(step, runs):
        source = lax.rem(me + owners - step, owners)

        @pl.when(source != me)
        def _():
            incoming(0, source).wait_recv()

        adds = []
        for h in range(heads):
            for i in range(per_source):
                ku = unit(k_all[rows_in(source, i), h * DK : (h + 1) * DK])
                k_all[rows_in(source, i), h * DK : (h + 1) * DK] = ku
                adds.append(dot(ku, ku, (0, 0)))
        runs = list(runs)
        for h in range(heads):
            for i in range(per_source):
                sys_ref[h * groups + source * per_source + i] = adds[h * per_source + i]
                runs[h] = runs[h] + adds[h * per_source + i]
        return tuple(runs)

    zero = tuple(jnp.zeros((DK, DK), F32) for _ in range(heads))
    runs = lax.fori_loop(0, owners, keys_in, zero)
    for h in range(heads):
        gram_total[h] = runs[h]
    chain(gram_total, gram_staged, gram_before, gram_send, gram_recv)

    def values_in(source, runs):
        @pl.when(source != me)
        def _():
            incoming(1, source).wait_recv()

        adds = []
        for h in range(heads):
            for i in range(per_source):
                cols = slice(h * DK, (h + 1) * DK)
                adds.append(dot(k_all[rows_in(source, i), cols], v_all[rows_in(source, i), cols], (0, 0)))
        runs = list(runs)
        for h in range(heads):
            for i in range(per_source):
                vk_ref[h * groups + source * per_source + i] = runs[h]
                runs[h] = runs[h] + adds[h * per_source + i]
        return tuple(runs)

    def values_out():
        runs = lax.fori_loop(0, owners, values_in, zero)
        for h in range(heads):
            vk_total[h] = runs[h]
        chain(vk_total, vk_staged, vk_before, vk_send, vk_recv)

    eye = lax.broadcasted_iota(jnp.int32, (DK, DK), 0) == lax.broadcasted_iota(jnp.int32, (DK, DK), 1)

    def start_of(c, runs):
        runs = list(runs)
        for h in range(heads):
            own_gram = sys_ref[h * groups + c]
            sys_ref[h * groups + c] = runs[h]
            runs[h] = runs[h] + own_gram
        return tuple(runs)

    lax.fori_loop(
        0, groups, start_of,
        tuple(gram_before[h] + jnp.where(eye, ridge_ref[pl.ds(me * heads + h, 1), :], 0.0) for h in range(heads)),
    )

    invert_all(sys_ref, pinv_ref, values_out)

    for step in range(1, owners):
        incoming(2, lax.rem(me + step, owners)).wait_recv()

    def result_copy(peer):
        return pltpu.make_async_remote_copy(
            src_ref=stage.at[peer],
            dst_ref=out_hbm.at[:, cols_of(me)],
            send_sem=out_send.at[peer],
            recv_sem=out_recv.at[me],
            device_id={"head": peer},
            device_id_type=pl.DeviceIdType.MESH,
        )

    sub = lax.broadcasted_iota(jnp.int32, (GROUP, 2 * GROUP), 0)
    lane = lax.broadcasted_iota(jnp.int32, (GROUP, 2 * GROUP), 1)
    twice = lane >= GROUP
    causal = jnp.where(twice, lane - GROUP, lane) <= sub

    def finish(step, carry):
        source = lax.rem(me + 1 + step, owners)
        jobs = [(h, i) for h in range(heads) for i in range(per_source)]
        solved = []
        for h, i in jobs:
            qu = unit(q_all[rows_in(source, i), h * DK : (h + 1) * DK])
            full = jnp.concatenate(split3(sys_ref[h * groups + source * per_source + i]), axis=0)
            solved.append(split3(-dot(jnp.concatenate([qu, qu, qu], axis=1), full, (1, 0))))
        scores, carried = [], []
        for (h, i), (high, mid, low) in zip(jobs, solved):
            ku = k_all[rows_in(source, i), h * DK : (h + 1) * DK]
            ku = jnp.concatenate([ku, ku], axis=0)
            ku = jnp.concatenate([ku, ku, ku], axis=1)
            scores.append(dot(jnp.concatenate([high, mid, low], axis=1), ku, (1, 1)))
            left = jnp.concatenate([high, high, mid, high, low, mid], axis=1)
            start = vk_ref[h * groups + source * per_source + i] + vk_before[h]
            carried.append(dot(left, right_stack(split3(start)), (1, 0)))
        for (h, i), score, carry_in in zip(jobs, scores, carried):
            score = jnp.where(causal, score, 0.0)
            high = score.astype(BF16).astype(F32)
            both = jnp.where(twice, score - high, high).astype(BF16)
            vb = v_all[rows_in(source, i), h * DK : (h + 1) * DK]
            inner = dot(both, jnp.concatenate([vb, vb], axis=0), (1, 0))
            stage[source, i * GROUP : (i + 1) * GROUP, h * DK : (h + 1) * DK] = (carry_in + inner).astype(BF16)

        @pl.when(source != me)
        def _():
            result_copy(source).start()

        return carry

    lax.fori_loop(0, owners, finish, 0)
    mine = pltpu.make_async_copy(stage.at[me], out_hbm.at[:, cols_of(me)], out_local)
    mine.start()
    for step in range(1, owners):
        peer = lax.rem(me + step, owners)
        for kind in range(3):
            outgoing(kind, peer).wait_send()
        result_copy(peer).wait_send()
    for step in range(1, owners):
        source = lax.rem(me + step, owners)
        pltpu.make_async_remote_copy(
            src_ref=stage.at[source],
            dst_ref=out_hbm.at[:, cols_of(source)],
            send_sem=out_send.at[source],
            recv_sem=out_recv.at[source],
            device_id={"head": source},
            device_id_type=pl.DeviceIdType.MESH,
        ).wait_recv()
    mine.wait()
    drain(gram_staged, gram_before, gram_send, gram_recv)
    drain(vk_staged, vk_before, vk_send, vk_recv)


def body(queries, key_rows, value_rows, ridge_diag):
    owners, shards = lax.axis_size("head"), lax.axis_size("seq")
    rows, columns = queries.shape
    width = columns // owners
    heads = width // DK
    tokens = rows * owners
    systems = heads * (tokens // GROUP)
    anywhere = pl.BlockSpec(memory_space=pltpu.HBM)
    dma = pltpu.SemaphoreType.DMA
    return pl.pallas_call(
        functools.partial(whole_kernel, owners, shards),
        out_shape=jax.ShapeDtypeStruct((rows, columns), BF16),
        in_specs=[anywhere] * 3 + [pl.BlockSpec(memory_space=pltpu.VMEM)],
        out_specs=anywhere,
        scratch_shapes=[
            pltpu.VMEM((tokens, width), BF16),
            pltpu.VMEM((tokens, width), BF16),
            pltpu.VMEM((tokens, width), BF16),
            pltpu.VMEM((systems, DK, DK), F32),
            pltpu.VMEM((systems, DK, DK), F32),
            pltpu.VMEM((systems // PACK, EDGE, DK), F32),
            pltpu.VMEM((owners, rows, width), BF16),
            *[pltpu.VMEM((heads, DK, DK), F32)] * 6,
            dma((3, owners)), dma((3, owners)), dma((3,)),
            dma((owners,)), dma((owners,)), dma,
            *[dma((heads * DK // CHUNK,))] * 4,
        ],
        compiler_params=pltpu.CompilerParams(
            vmem_limit_bytes=67_000_000, collective_id=0, has_side_effects=True
        ),
    )(queries, key_rows, value_rows, ridge_diag)


def solution(mesh):
    in_specs = (P(("seq", "head"), None), P(("seq", "head"), None), P(("seq", "head"), None), P())
    out_specs = P(("seq", "head"), None)
    return jax.shard_map(body, mesh=mesh, in_specs=in_specs, out_specs=out_specs, check_vma=False)
```

```python
import functools

import jax
import jax.numpy as jnp
from jax import lax
from jax.experimental import pallas as pl
from jax.experimental.pallas import tpu as pltpu
from jax.sharding import PartitionSpec as P

DK = 128
GROUP = 64
EDGE = 32
BATCH = 16
SUBLANES = 8
CHUNK = 64
EPS = 1e-06
F32 = jnp.float32
BF16 = jnp.bfloat16


def unit(rows):
    wide = rows.astype(F32)
    back = lax.rsqrt(jnp.sum(wide * wide, axis=-1, keepdims=True) + EPS)
    return (wide * back).astype(BF16)


def split3(value):
    high = value.astype(BF16)
    rest = value - high.astype(F32)
    mid = rest.astype(BF16)
    low = (rest - mid.astype(F32)).astype(BF16)
    return high, mid, low


def dot(left, right, contract):
    return lax.dot_general(left, right, ((contract[:1], contract[1:]), ((), ())), preferred_element_type=F32)


def left_stack(parts):
    high, mid, low = parts
    return jnp.concatenate([high, high, mid, high, low, mid], axis=0)


def right_stack(parts):
    high, mid, low = parts
    return jnp.concatenate([high, mid, high, low, high, mid], axis=0)


def sweep_pair(tiles, turn, lane, sub):
    at, inner = turn // SUBLANES, turn % SUBLANES
    within = lane % SUBLANES
    pick1 = lane - within + inner
    pick2 = pick1 + 1
    first, second = within == inner, within == inner + 1
    either = jnp.logical_or(first, second)
    here1, here2 = sub == inner, sub == inner + 1
    here = jnp.logical_or(here1, here2)

    def take(block, pick):
        return jnp.take_along_axis(block, pick, axis=1, mode="promise_in_bounds")

    def spread(block, row):
        return jnp.broadcast_to(block[row : row + 1, :], block.shape)

    col1 = [take(block, pick1) for block in tiles[at]]
    col2 = [take(block, pick2) for block in tiles[at]]
    a, b, d = spread(col1[at], inner), spread(col2[at], inner), spread(col2[at], inner + 1)
    back = 1.0 / (a * d - b * b)
    e, f, h = d * back, b * back, a * back
    col1[at] = jnp.where(here1, -1.0, jnp.where(here2, 0.0, col1[at]))
    col2[at] = jnp.where(here2, -1.0, jnp.where(here1, 0.0, col2[at]))
    fresh = []
    for g, column in enumerate(tiles):
        row1, row2 = spread(column[at], inner), spread(column[at], inner + 1)
        if g == at:
            row1 = jnp.where(first, -1.0, jnp.where(second, 0.0, row1))
            row2 = jnp.where(second, -1.0, jnp.where(first, 0.0, row2))
        scaled1, scaled2 = e * row1 - f * row2, h * row2 - f * row1
        blocks = []
        for v, block in enumerate(column):
            if v == at:
                block = jnp.where(here, 0.0, block)
            if g == at:
                block = jnp.where(either, 0.0, block)
            blocks.append(block - (col1[v] * scaled1 + col2[v] * scaled2))
        fresh.append(blocks)
    return fresh


def invert_all(count, sys_ref, turn_ref, pinv_ref, midway):
    copies = DK // EDGE
    share = DK // SUBLANES
    bands = EDGE // SUBLANES
    lane = lax.broadcasted_iota(jnp.int32, (SUBLANES, DK), 1)
    sub = lax.broadcasted_iota(jnp.int32, (SUBLANES, DK), 0)
    lane32 = lax.broadcasted_iota(jnp.int32, (EDGE, DK), 1)
    sub32 = lax.broadcasted_iota(jnp.int32, (EDGE, DK), 0)
    row128 = lax.broadcasted_iota(jnp.int32, (DK, DK), 0) // EDGE
    lane128 = lax.broadcasted_iota(jnp.int32, (DK, DK), 1) // EDGE

    def panel(p, carry):
        @pl.when(p == copies // 2)
        def _():
            midway()

        start = pl.multiple_of(p * EDGE, EDGE)
        halves = []
        for half in range(count // share):
            tiles = []
            for g in range(bands):
                at = half * bands + g
                stacked = [
                    sys_ref[pl.ds(pl.multiple_of((half * share + s) * DK + start + g * SUBLANES, SUBLANES), SUBLANES), :]
                    for s in range(share)
                ]
                turn_ref[at] = jnp.transpose(jnp.concatenate(stacked, axis=0))
                tiles.append([
                    turn_ref[at, pl.ds(pl.multiple_of(start + v * SUBLANES, SUBLANES), SUBLANES), :] for v in range(bands)
                ])
            halves.append(tiles)
        for turn in range(0, EDGE, 2):
            halves = [sweep_pair(tiles, turn, lane, sub) for tiles in halves]
        for half, tiles in enumerate(halves):
            for g, column in enumerate(tiles):
                block = jnp.transpose(jnp.concatenate(column * copies, axis=0))
                for s in range(share):
                    row = (half * share + s) * EDGE + g * SUBLANES
                    pinv_ref[row : row + SUBLANES, :] = block[s * SUBLANES : (s + 1) * SUBLANES, :]

        mine = lane32 // EDGE == p
        diag = lane32 - p * EDGE == sub32
        cleared = jnp.logical_or(row128 == p, lane128 == p)
        third = lane32 // EDGE == 2
        first = lane32 // EDGE == 0

        def update(turn, carry):
            batch = [turn * BATCH + i for i in range(BATCH)]
            lefts, rows = [], []
            for g in batch:
                high, mid, low = split3(pinv_ref[pl.ds(pl.multiple_of(g * EDGE, EDGE), EDGE), :])
                left = jnp.concatenate([jnp.where(third, mid, high), jnp.where(first, low, mid)], axis=1)
                lefts.append(left[:, : 6 * EDGE])
                row = sys_ref[pl.ds(pl.multiple_of(g * DK, DK) + start, EDGE), :]
                rows.append(split3(jnp.where(mine, jnp.where(diag, -1.0, 0.0), row)))
            scaled = [dot(left, right_stack(r), (1, 0)) for left, r in zip(lefts, rows)]
            change = [dot(left_stack(r), right_stack(split3(t)), (0, 0)) for r, t in zip(rows, scaled)]
            for g, c in zip(batch, change):
                whole = pl.ds(pl.multiple_of(g * DK, DK), DK)
                sys_ref[whole, :] = jnp.where(cleared, 0.0, sys_ref[whole, :]) + c
            return carry

        return lax.fori_loop(0, count // BATCH, update, carry)

    lax.fori_loop(0, copies, panel, 0)


def whole_kernel(
    owners, shards, q_hbm, k_hbm, v_hbm, ridge_ref, out_hbm,
    q_all, k_all, v_all, sys_ref, vk_ref, turn_ref, pinv_ref, stage, gram_total, vk_total, gram_staged, vk_staged, gram_before, vk_before,
    send_sems, recv_sems, local_sems, out_send, out_recv, out_local, gram_send, gram_recv, vk_send, vk_recv,
):
    me, shard = lax.axis_index("head"), lax.axis_index("seq")
    rows_each = q_hbm.shape[0]
    width = q_all.shape[1]
    heads = width // DK
    per_source = rows_each // GROUP
    groups = owners * per_source
    moved = ((k_hbm, k_all), (v_hbm, v_all), (q_hbm, q_all))

    def rows_of(source):
        return pl.ds(pl.multiple_of(source * rows_each, rows_each), rows_each)

    def cols_of(owner):
        return pl.ds(pl.multiple_of(owner * width, width), width)

    def incoming(kind, source):
        return pltpu.make_async_remote_copy(
            src_ref=moved[kind][0].at[:, cols_of(source)],
            dst_ref=moved[kind][1].at[rows_of(source), :],
            send_sem=send_sems.at[kind, source],
            recv_sem=recv_sems.at[kind, source],
            device_id={"head": source},
            device_id_type=pl.DeviceIdType.MESH,
        )

    def outgoing(kind, peer):
        return pltpu.make_async_remote_copy(
            src_ref=moved[kind][0].at[:, cols_of(peer)],
            dst_ref=moved[kind][1].at[rows_of(me), :],
            send_sem=send_sems.at[kind, peer],
            recv_sem=recv_sems.at[kind, me],
            device_id={"head": peer},
            device_id_type=pl.DeviceIdType.MESH,
        )

    def own(kind):
        return pltpu.make_async_copy(
            moved[kind][0].at[:, cols_of(me)], moved[kind][1].at[rows_of(me), :], local_sems.at[kind]
        )

    def chunk(c):
        return c * CHUNK // DK, pl.ds(c * CHUNK % DK, CHUNK)

    def link_copy(staged, before, send, recv, c, target):
        head, rows = chunk(c)
        return pltpu.make_async_remote_copy(
            src_ref=staged.at[head, rows, :],
            dst_ref=before.at[head, rows, :],
            send_sem=send.at[c],
            recv_sem=recv.at[c],
            device_id={"seq": target},
            device_id_type=pl.DeviceIdType.MESH,
        )

    chunks = heads * DK // CHUNK

    def chain(total, staged, before, send, recv):
        for c in range(chunks):
            head, rows = chunk(c)

            @pl.when(shard > 0)
            def _():
                link_copy(staged, before, send, recv, c, shard).wait_recv()

            @pl.when(shard + 1 < shards)
            def _():
                staged[head, rows, :] = total[head, rows, :] + before[head, rows, :]
                link_copy(staged, before, send, recv, c, shard + 1).start()

    def drain(staged, before, send, recv):
        for c in range(chunks):
            @pl.when(shard + 1 < shards)
            def _():
                link_copy(staged, before, send, recv, c, shard + 1).wait_send()

    barrier = pltpu.get_barrier_semaphore()
    for step in range(1, owners):
        pl.semaphore_signal(barrier, inc=1, device_id={"head": lax.rem(me + step, owners)}, device_id_type=pl.DeviceIdType.MESH)
    for near in (shard - 1, shard + 1):
        @pl.when(jnp.logical_and(near >= 0, near < shards))
        def _():
            pl.semaphore_signal(barrier, inc=1, device_id={"seq": near}, device_id_type=pl.DeviceIdType.MESH)
    for kind in range(3):
        own(kind).start()
    ends = (shard == 0).astype(jnp.int32) + (shard == shards - 1).astype(jnp.int32)
    pl.semaphore_wait(barrier, owners - 1 + 2 - ends)
    for kind in range(3):
        for step in range(1, owners):
            outgoing(kind, lax.rem(me + step, owners)).start()
    for kind in range(3):
        own(kind).wait()

    @pl.when(shard == 0)
    def _():
        gram_before[...] = jnp.zeros_like(gram_before)
        vk_before[...] = jnp.zeros_like(vk_before)

    def system(head, group):
        return pl.ds(pl.multiple_of((head * groups + group) * DK, DK), DK)

    def rows_in(source, i):
        return pl.ds(pl.multiple_of(source * rows_each + i * GROUP, GROUP), GROUP)

    def keys_in(step, runs):
        source = lax.rem(me + owners - step, owners)

        @pl.when(source != me)
        def _():
            incoming(0, source).wait_recv()

        adds = []
        for h in range(heads):
            for i in range(per_source):
                ku = unit(k_all[rows_in(source, i), h * DK : (h + 1) * DK])
                k_all[rows_in(source, i), h * DK : (h + 1) * DK] = ku
                adds.append(dot(ku, ku, (0, 0)))
        runs = list(runs)
        for h in range(heads):
            for i in range(per_source):
                sys_ref[system(h, source * per_source + i), :] = adds[h * per_source + i]
                runs[h] = runs[h] + adds[h * per_source + i]
        return tuple(runs)

    zero = tuple(jnp.zeros((DK, DK), F32) for _ in range(heads))
    runs = lax.fori_loop(0, owners, keys_in, zero)
    for h in range(heads):
        gram_total[h] = runs[h]
    chain(gram_total, gram_staged, gram_before, gram_send, gram_recv)

    def values_in(source, runs):
        @pl.when(source != me)
        def _():
            incoming(1, source).wait_recv()

        adds = []
        for h in range(heads):
            for i in range(per_source):
                cols = slice(h * DK, (h + 1) * DK)
                adds.append(dot(k_all[rows_in(source, i), cols], v_all[rows_in(source, i), cols], (0, 0)))
        runs = list(runs)
        for h in range(heads):
            for i in range(per_source):
                vk_ref[h * groups + source * per_source + i] = runs[h]
                runs[h] = runs[h] + adds[h * per_source + i]
        return tuple(runs)

    def values_out():
        runs = lax.fori_loop(0, owners, values_in, zero)
        for h in range(heads):
            vk_total[h] = runs[h]
        chain(vk_total, vk_staged, vk_before, vk_send, vk_recv)

    eye = lax.broadcasted_iota(jnp.int32, (DK, DK), 0) == lax.broadcasted_iota(jnp.int32, (DK, DK), 1)

    def start_of(c, runs):
        runs = list(runs)
        for h in range(heads):
            own_gram = sys_ref[system(h, c), :]
            sys_ref[system(h, c), :] = runs[h]
            runs[h] = runs[h] + own_gram
        return tuple(runs)

    lax.fori_loop(
        0, groups, start_of,
        tuple(gram_before[h] + jnp.where(eye, ridge_ref[pl.ds(me * heads + h, 1), :], 0.0) for h in range(heads)),
    )

    invert_all(heads * groups, sys_ref, turn_ref, pinv_ref, values_out)

    for step in range(1, owners):
        incoming(2, lax.rem(me + step, owners)).wait_recv()

    def result_copy(peer):
        return pltpu.make_async_remote_copy(
            src_ref=stage.at[peer],
            dst_ref=out_hbm.at[:, cols_of(me)],
            send_sem=out_send.at[peer],
            recv_sem=out_recv.at[me],
            device_id={"head": peer},
            device_id_type=pl.DeviceIdType.MESH,
        )

    sub = lax.broadcasted_iota(jnp.int32, (GROUP, 2 * GROUP), 0)
    lane = lax.broadcasted_iota(jnp.int32, (GROUP, 2 * GROUP), 1)
    twice = lane >= GROUP
    causal = jnp.where(twice, lane - GROUP, lane) <= sub

    def finish(step, carry):
        source = lax.rem(me + 1 + step, owners)
        jobs = [(h, i) for h in range(heads) for i in range(per_source)]
        solved = []
        for h, i in jobs:
            qu = unit(q_all[rows_in(source, i), h * DK : (h + 1) * DK])
            full = jnp.concatenate(split3(sys_ref[system(h, source * per_source + i), :]), axis=0)
            solved.append(split3(-dot(jnp.concatenate([qu, qu, qu], axis=1), full, (1, 0))))
        scores, carried = [], []
        for (h, i), (high, mid, low) in zip(jobs, solved):
            ku = k_all[rows_in(source, i), h * DK : (h + 1) * DK]
            ku = jnp.concatenate([ku, ku], axis=0)
            ku = jnp.concatenate([ku, ku, ku], axis=1)
            scores.append(dot(jnp.concatenate([high, mid, low], axis=1), ku, (1, 1)))
            left = jnp.concatenate([high, high, mid, high, low, mid], axis=1)
            start = vk_ref[h * groups + source * per_source + i] + vk_before[h]
            carried.append(dot(left, right_stack(split3(start)), (1, 0)))
        for (h, i), score, carry_in in zip(jobs, scores, carried):
            score = jnp.where(causal, score, 0.0)
            high = score.astype(BF16).astype(F32)
            both = jnp.where(twice, score - high, high).astype(BF16)
            vb = v_all[rows_in(source, i), h * DK : (h + 1) * DK]
            inner = dot(both, jnp.concatenate([vb, vb], axis=0), (1, 0))
            stage[source, i * GROUP : (i + 1) * GROUP, h * DK : (h + 1) * DK] = (carry_in + inner).astype(BF16)

        @pl.when(source != me)
        def _():
            result_copy(source).start()

        return carry

    lax.fori_loop(0, owners, finish, 0)
    mine = pltpu.make_async_copy(stage.at[me], out_hbm.at[:, cols_of(me)], out_local)
    mine.start()
    for step in range(1, owners):
        peer = lax.rem(me + step, owners)
        for kind in range(3):
            outgoing(kind, peer).wait_send()
        result_copy(peer).wait_send()
    for step in range(1, owners):
        source = lax.rem(me + step, owners)
        pltpu.make_async_remote_copy(
            src_ref=stage.at[source],
            dst_ref=out_hbm.at[:, cols_of(source)],
            send_sem=out_send.at[source],
            recv_sem=out_recv.at[source],
            device_id={"head": source},
            device_id_type=pl.DeviceIdType.MESH,
        ).wait_recv()
    mine.wait()
    drain(gram_staged, gram_before, gram_send, gram_recv)
    drain(vk_staged, vk_before, vk_send, vk_recv)


def body(queries, key_rows, value_rows, ridge_diag):
    owners, shards = lax.axis_size("head"), lax.axis_size("seq")
    rows, columns = queries.shape
    width = columns // owners
    heads = width // DK
    tokens = rows * owners
    systems = heads * (tokens // GROUP)
    anywhere = pl.BlockSpec(memory_space=pltpu.HBM)
    dma = pltpu.SemaphoreType.DMA
    return pl.pallas_call(
        functools.partial(whole_kernel, owners, shards),
        out_shape=jax.ShapeDtypeStruct((rows, columns), BF16),
        in_specs=[anywhere] * 3 + [pl.BlockSpec(memory_space=pltpu.VMEM)],
        out_specs=anywhere,
        scratch_shapes=[
            pltpu.VMEM((tokens, width), BF16),
            pltpu.VMEM((tokens, width), BF16),
            pltpu.VMEM((tokens, width), BF16),
            pltpu.VMEM((systems * DK, DK), F32),
            pltpu.VMEM((systems, DK, DK), F32),
            pltpu.VMEM((systems * EDGE // DK, DK, DK), F32),
            pltpu.VMEM((systems * EDGE, DK), F32),
            pltpu.VMEM((owners, rows, width), BF16),
            *[pltpu.VMEM((heads, DK, DK), F32)] * 6,
            dma((3, owners)), dma((3, owners)), dma((3,)),
            dma((owners,)), dma((owners,)), dma,
            *[dma((heads * DK // CHUNK,))] * 4,
        ],
        compiler_params=pltpu.CompilerParams(
            vmem_limit_bytes=67_000_000, collective_id=0, has_side_effects=True
        ),
    )(queries, key_rows, value_rows, ridge_diag)


def solution(mesh):
    in_specs = (P(("seq", "head"), None), P(("seq", "head"), None), P(("seq", "head"), None), P())
    out_specs = P(("seq", "head"), None)
    return jax.shard_map(body, mesh=mesh, in_specs=in_specs, out_specs=out_specs, check_vma=False)
```

```python
import functools

import jax
import jax.numpy as jnp
from jax import lax
from jax.experimental import pallas as pl
from jax.experimental.pallas import tpu as pltpu
from jax.sharding import PartitionSpec as P

DK = 128
GROUP = 64
EDGE = 32
BATCH = 16
SUBLANES = 8
CHUNK = 64
EPS = 1e-06
F32 = jnp.float32
BF16 = jnp.bfloat16


def unit(rows):
    wide = rows.astype(F32)
    back = lax.rsqrt(jnp.sum(wide * wide, axis=-1, keepdims=True) + EPS)
    return (wide * back).astype(BF16)


def split3(value):
    high = value.astype(BF16)
    rest = value - high.astype(F32)
    mid = rest.astype(BF16)
    low = (rest - mid.astype(F32)).astype(BF16)
    return high, mid, low


def dot(left, right, contract):
    return lax.dot_general(left, right, ((contract[:1], contract[1:]), ((), ())), preferred_element_type=F32)


def left_stack(parts):
    high, mid, low = parts
    return jnp.concatenate([high, high, mid, high, low, mid], axis=0)


def right_stack(parts):
    high, mid, low = parts
    return jnp.concatenate([high, mid, high, low, high, mid], axis=0)


def sweep_pair(tiles, turn, lane, sub):
    at, inner = turn // SUBLANES, turn % SUBLANES
    within = lane % SUBLANES
    pick1 = lane - within + inner
    pick2 = pick1 + 1
    first, second = within == inner, within == inner + 1
    either = jnp.logical_or(first, second)
    here1, here2 = sub == inner, sub == inner + 1
    here = jnp.logical_or(here1, here2)

    def take(block, pick):
        return jnp.take_along_axis(block, pick, axis=1, mode="promise_in_bounds")

    def spread(block, row):
        return jnp.broadcast_to(block[row : row + 1, :], block.shape)

    col1 = [take(block, pick1) for block in tiles[at]]
    col2 = [take(block, pick2) for block in tiles[at]]
    a, b, d = spread(col1[at], inner), spread(col2[at], inner), spread(col2[at], inner + 1)
    back = 1.0 / (a * d - b * b)
    e, f, h = d * back, b * back, a * back
    col1[at] = jnp.where(here1, -1.0, jnp.where(here2, 0.0, col1[at]))
    col2[at] = jnp.where(here2, -1.0, jnp.where(here1, 0.0, col2[at]))
    fresh = []
    for g, column in enumerate(tiles):
        row1, row2 = spread(column[at], inner), spread(column[at], inner + 1)
        if g == at:
            row1 = jnp.where(first, -1.0, jnp.where(second, 0.0, row1))
            row2 = jnp.where(second, -1.0, jnp.where(first, 0.0, row2))
        scaled1, scaled2 = e * row1 - f * row2, h * row2 - f * row1
        blocks = []
        for v, block in enumerate(column):
            if v == at:
                block = jnp.where(here, 0.0, block)
            if g == at:
                block = jnp.where(either, 0.0, block)
            blocks.append(block - (col1[v] * scaled1 + col2[v] * scaled2))
        fresh.append(blocks)
    return fresh


def invert_all(count, sys_ref, turn_ref, pinv_ref, midway):
    copies = DK // EDGE
    share = DK // SUBLANES
    bands = EDGE // SUBLANES
    lane = lax.broadcasted_iota(jnp.int32, (SUBLANES, DK), 1)
    sub = lax.broadcasted_iota(jnp.int32, (SUBLANES, DK), 0)
    lane32 = lax.broadcasted_iota(jnp.int32, (EDGE, DK), 1)
    sub32 = lax.broadcasted_iota(jnp.int32, (EDGE, DK), 0)
    row128 = lax.broadcasted_iota(jnp.int32, (DK, DK), 0) // EDGE
    lane128 = lax.broadcasted_iota(jnp.int32, (DK, DK), 1) // EDGE

    def panel(p, carry):
        @pl.when(p == copies // 2)
        def _():
            midway()

        start = pl.multiple_of(p * EDGE, EDGE)
        halves = []
        for half in range(count // share):
            tiles = []
            for g in range(bands):
                at = half * bands + g
                stacked = [
                    sys_ref[pl.ds(pl.multiple_of((half * share + s) * DK + start + g * SUBLANES, SUBLANES), SUBLANES), :]
                    for s in range(share)
                ]
                turn_ref[at] = jnp.transpose(jnp.concatenate(stacked, axis=0))
                tiles.append([
                    turn_ref[at, pl.ds(pl.multiple_of(start + v * SUBLANES, SUBLANES), SUBLANES), :] for v in range(bands)
                ])
            halves.append(tiles)
        for turn in range(0, EDGE, 2):
            halves = [sweep_pair(tiles, turn, lane, sub) for tiles in halves]
        for half, tiles in enumerate(halves):
            for g, column in enumerate(tiles):
                block = jnp.transpose(jnp.concatenate(column * copies, axis=0))
                for s in range(share):
                    row = (half * share + s) * EDGE + g * SUBLANES
                    pinv_ref[row : row + SUBLANES, :] = block[s * SUBLANES : (s + 1) * SUBLANES, :]

        mine = lane32 // EDGE == p
        diag = lane32 - p * EDGE == sub32
        cleared = jnp.logical_or(row128 == p, lane128 == p)
        third = lane32 // EDGE == 2
        first = lane32 // EDGE == 0

        def update(turn, carry):
            batch = [turn * BATCH + i for i in range(BATCH)]
            lefts, rows = [], []
            for g in batch:
                high, mid, low = split3(pinv_ref[pl.ds(pl.multiple_of(g * EDGE, EDGE), EDGE), :])
                left = jnp.concatenate([jnp.where(third, mid, high), jnp.where(first, low, mid)], axis=1)
                lefts.append(left[:, : 6 * EDGE])
                row = sys_ref[pl.ds(pl.multiple_of(g * DK, DK) + start, EDGE), :]
                rows.append(split3(jnp.where(mine, jnp.where(diag, -1.0, 0.0), row)))
            scaled = [dot(left, right_stack(r), (1, 0)) for left, r in zip(lefts, rows)]
            change = [dot(left_stack(r), right_stack(split3(t)), (0, 0)) for r, t in zip(rows, scaled)]
            for g, c in zip(batch, change):
                whole = pl.ds(pl.multiple_of(g * DK, DK), DK)
                sys_ref[whole, :] = jnp.where(cleared, 0.0, sys_ref[whole, :]) + c
            return carry

        return lax.fori_loop(0, count // BATCH, update, carry)

    lax.fori_loop(0, copies, panel, 0)


def whole_kernel(
    owners, shards, q_hbm, k_hbm, v_hbm, ridge_ref, out_hbm,
    q_all, k_all, v_all, sys_ref, vk_ref, turn_ref, pinv_ref, stage, gram_total, vk_total, gram_staged, vk_staged, gram_before, vk_before,
    send_sems, recv_sems, local_sems, out_send, out_recv, out_local, gram_send, gram_recv, vk_send, vk_recv,
):
    me, shard = lax.axis_index("head"), lax.axis_index("seq")
    rows_each = q_hbm.shape[0]
    width = q_all.shape[1]
    heads = width // DK
    per_source = rows_each // GROUP
    groups = owners * per_source
    moved = [(k_hbm, k_all, h * DK, DK) for h in range(heads)]
    moved += [(v_hbm, v_all, 0, width), (q_hbm, q_all, 0, width)]
    values, queries = heads, heads + 1
    middle = sorted(range(2, owners - 1), key=lambda step: abs(step - owners // 2))
    odd = lax.rem(me, 2)
    partner = owners - 1 - odd * (owners - 2)

    def pick(order, at):
        step = order[-1]
        for i, choice in enumerate(order[:-1]):
            step = jnp.where(at == i, choice, step)
        return step

    order_out = [*middle, partner, owners - partner]
    order_in = [0, owners - partner, *middle, partner]

    def rows_of(source):
        return pl.ds(pl.multiple_of(source * rows_each, rows_each), rows_each)

    def cols_of(owner):
        return pl.ds(pl.multiple_of(owner * width, width), width)

    def source_part(kind, owner):
        ref, _, offset, size = moved[kind]
        return ref.at[:, pl.ds(pl.multiple_of(owner * width + offset, size), size)]

    def target_part(kind, source):
        _, ref, offset, size = moved[kind]
        return ref.at[rows_of(source), pl.ds(offset, size)]

    def incoming(kind, source):
        return pltpu.make_async_remote_copy(
            src_ref=source_part(kind, source),
            dst_ref=target_part(kind, source),
            send_sem=send_sems.at[kind, source],
            recv_sem=recv_sems.at[kind, source],
            device_id={"head": source},
            device_id_type=pl.DeviceIdType.MESH,
        )

    def outgoing(kind, peer):
        return pltpu.make_async_remote_copy(
            src_ref=source_part(kind, peer),
            dst_ref=target_part(kind, me),
            send_sem=send_sems.at[kind, peer],
            recv_sem=recv_sems.at[kind, me],
            device_id={"head": peer},
            device_id_type=pl.DeviceIdType.MESH,
        )

    def own(kind):
        return pltpu.make_async_copy(source_part(kind, me), target_part(kind, me), local_sems.at[kind])

    def chunk(c):
        return c * CHUNK // DK, pl.ds(c * CHUNK % DK, CHUNK)

    def link_copy(staged, before, send, recv, c, target):
        head, rows = chunk(c)
        return pltpu.make_async_remote_copy(
            src_ref=staged.at[head, rows, :],
            dst_ref=before.at[head, rows, :],
            send_sem=send.at[c],
            recv_sem=recv.at[c],
            device_id={"seq": target},
            device_id_type=pl.DeviceIdType.MESH,
        )

    chunks = heads * DK // CHUNK

    def pass_on(total, staged, before, send, recv, only=None):
        for c in range(chunks):
            head, rows = chunk(c)
            if only in (None, head):
                staged[head, rows, :] = total[head, rows, :] + before[head, rows, :]
                link_copy(staged, before, send, recv, c, shard + 1).start()

    def chain(total, staged, before, send, recv):
        for c in range(chunks):
            head, rows = chunk(c)
            link_copy(staged, before, send, recv, c, shard).wait_recv()

            @pl.when(shard + 1 < shards)
            def _():
                staged[head, rows, :] = total[head, rows, :] + before[head, rows, :]
                link_copy(staged, before, send, recv, c, shard + 1).start()

    def drain(staged, before, send, recv):
        for c in range(chunks):
            @pl.when(shard + 1 < shards)
            def _():
                link_copy(staged, before, send, recv, c, shard + 1).wait_send()

    barrier = pltpu.get_barrier_semaphore()
    for step in range(1, owners):
        pl.semaphore_signal(barrier, inc=1, device_id={"head": lax.rem(me + step, owners)}, device_id_type=pl.DeviceIdType.MESH)
    for near in (shard - 1, shard + 1):
        @pl.when(jnp.logical_and(near >= 0, near < shards))
        def _():
            pl.semaphore_signal(barrier, inc=1, device_id={"seq": near}, device_id_type=pl.DeviceIdType.MESH)
    for kind in range(len(moved)):
        own(kind).start()
    ends = (shard == 0).astype(jnp.int32) + (shard == shards - 1).astype(jnp.int32)
    pl.semaphore_wait(barrier, owners - 1 + 2 - ends)
    for kind in range(len(moved)):
        for step in order_out:
            outgoing(kind, lax.rem(me + step, owners)).start()
    for kind in range(len(moved)):
        own(kind).wait()

    @pl.when(shard == 0)
    def _():
        gram_before[...] = jnp.zeros_like(gram_before)
        vk_before[...] = jnp.zeros_like(vk_before)

    def system(head, group):
        return pl.ds(pl.multiple_of((head * groups + group) * DK, DK), DK)

    def rows_in(source, i):
        return pl.ds(pl.multiple_of(source * rows_each + i * GROUP, GROUP), GROUP)

    def keys_of(h):
        cols = slice(h * DK, (h + 1) * DK)

        def keys_in(at, run):
            source = lax.rem(me + owners - pick(order_in, at), owners)

            @pl.when(source != me)
            def _():
                incoming(h, source).wait_recv()

            adds = []
            for i in range(per_source):
                ku = unit(k_all[rows_in(source, i), cols])
                k_all[rows_in(source, i), cols] = ku
                adds.append(dot(ku, ku, (0, 0)))
            for i in range(per_source):
                sys_ref[system(h, source * per_source + i), :] = adds[i]
                run = run + adds[i]
            return run

        gram_total[h] = lax.fori_loop(0, owners, keys_in, jnp.zeros((DK, DK), F32))

    zero = tuple(jnp.zeros((DK, DK), F32) for _ in range(heads))
    for h in range(heads):
        keys_of(h)

        @pl.when(shard == 0)
        def _():
            pass_on(gram_total, gram_staged, gram_before, gram_send, gram_recv, h)

    @pl.when(shard > 0)
    def _():
        chain(gram_total, gram_staged, gram_before, gram_send, gram_recv)


    def values_in(source, runs):
        @pl.when(source != me)
        def _():
            incoming(values, source).wait_recv()

        adds = []
        for h in range(heads):
            for i in range(per_source):
                cols = slice(h * DK, (h + 1) * DK)
                adds.append(dot(k_all[rows_in(source, i), cols], v_all[rows_in(source, i), cols], (0, 0)))
        runs = list(runs)
        for h in range(heads):
            for i in range(per_source):
                vk_ref[h * groups + source * per_source + i] = runs[h]
                runs[h] = runs[h] + adds[h * per_source + i]
        return tuple(runs)

    def values_out():
        runs = lax.fori_loop(0, owners, values_in, zero)
        for h in range(heads):
            vk_total[h] = runs[h]

        @pl.when(shard == 0)
        def _():
            pass_on(vk_total, vk_staged, vk_before, vk_send, vk_recv)

        @pl.when(shard > 0)
        def _():
            chain(vk_total, vk_staged, vk_before, vk_send, vk_recv)

    eye = lax.broadcasted_iota(jnp.int32, (DK, DK), 0) == lax.broadcasted_iota(jnp.int32, (DK, DK), 1)

    def start_of(c, runs):
        runs = list(runs)
        for h in range(heads):
            own_gram = sys_ref[system(h, c), :]
            sys_ref[system(h, c), :] = runs[h]
            runs[h] = runs[h] + own_gram
        return tuple(runs)

    lax.fori_loop(
        0, groups, start_of,
        tuple(gram_before[h] + jnp.where(eye, ridge_ref[pl.ds(me * heads + h, 1), :], 0.0) for h in range(heads)),
    )

    invert_all(heads * groups, sys_ref, turn_ref, pinv_ref, values_out)

    for step in range(1, owners):
        incoming(queries, lax.rem(me + step, owners)).wait_recv()

    def result_copy(peer):
        return pltpu.make_async_remote_copy(
            src_ref=stage.at[peer],
            dst_ref=out_hbm.at[:, cols_of(me)],
            send_sem=out_send.at[peer],
            recv_sem=out_recv.at[me],
            device_id={"head": peer},
            device_id_type=pl.DeviceIdType.MESH,
        )

    sub = lax.broadcasted_iota(jnp.int32, (GROUP, 2 * GROUP), 0)
    lane = lax.broadcasted_iota(jnp.int32, (GROUP, 2 * GROUP), 1)
    twice = lane >= GROUP
    causal = jnp.where(twice, lane - GROUP, lane) <= sub

    def finish(step, carry):
        source = lax.rem(me + pick([*order_out, 0], step), owners)
        jobs = [(h, i) for h in range(heads) for i in range(per_source)]
        solved = []
        for h, i in jobs:
            qu = unit(q_all[rows_in(source, i), h * DK : (h + 1) * DK])
            full = jnp.concatenate(split3(sys_ref[system(h, source * per_source + i), :]), axis=0)
            solved.append(split3(-dot(jnp.concatenate([qu, qu, qu], axis=1), full, (1, 0))))
        scores, carried = [], []
        for (h, i), (high, mid, low) in zip(jobs, solved):
            ku = k_all[rows_in(source, i), h * DK : (h + 1) * DK]
            ku = jnp.concatenate([ku, ku], axis=0)
            ku = jnp.concatenate([ku, ku, ku], axis=1)
            scores.append(dot(jnp.concatenate([high, mid, low], axis=1), ku, (1, 1)))
            left = jnp.concatenate([high, high, mid, high, low, mid], axis=1)
            start = vk_ref[h * groups + source * per_source + i] + vk_before[h]
            carried.append(dot(left, right_stack(split3(start)), (1, 0)))
        for (h, i), score, carry_in in zip(jobs, scores, carried):
            score = jnp.where(causal, score, 0.0)
            high = score.astype(BF16).astype(F32)
            both = jnp.where(twice, score - high, high).astype(BF16)
            vb = v_all[rows_in(source, i), h * DK : (h + 1) * DK]
            inner = dot(both, jnp.concatenate([vb, vb], axis=0), (1, 0))
            stage[source, i * GROUP : (i + 1) * GROUP, h * DK : (h + 1) * DK] = (carry_in + inner).astype(BF16)

        @pl.when(source != me)
        def _():
            result_copy(source).start()

        return carry

    lax.fori_loop(0, owners, finish, 0)
    mine = pltpu.make_async_copy(stage.at[me], out_hbm.at[:, cols_of(me)], out_local)
    mine.start()
    for step in range(1, owners):
        peer = lax.rem(me + step, owners)
        for kind in range(len(moved)):
            outgoing(kind, peer).wait_send()
        result_copy(peer).wait_send()
    for step in range(1, owners):
        source = lax.rem(me + step, owners)
        pltpu.make_async_remote_copy(
            src_ref=stage.at[source],
            dst_ref=out_hbm.at[:, cols_of(source)],
            send_sem=out_send.at[source],
            recv_sem=out_recv.at[source],
            device_id={"head": source},
            device_id_type=pl.DeviceIdType.MESH,
        ).wait_recv()
    mine.wait()
    drain(gram_staged, gram_before, gram_send, gram_recv)
    drain(vk_staged, vk_before, vk_send, vk_recv)


def body(queries, key_rows, value_rows, ridge_diag):
    owners, shards = lax.axis_size("head"), lax.axis_size("seq")
    rows, columns = queries.shape
    width = columns // owners
    heads = width // DK
    tokens = rows * owners
    systems = heads * (tokens // GROUP)
    anywhere = pl.BlockSpec(memory_space=pltpu.HBM)
    dma = pltpu.SemaphoreType.DMA
    return pl.pallas_call(
        functools.partial(whole_kernel, owners, shards),
        out_shape=jax.ShapeDtypeStruct((rows, columns), BF16),
        in_specs=[anywhere] * 3 + [pl.BlockSpec(memory_space=pltpu.VMEM)],
        out_specs=anywhere,
        scratch_shapes=[
            pltpu.VMEM((tokens, width), BF16),
            pltpu.VMEM((tokens, width), BF16),
            pltpu.VMEM((tokens, width), BF16),
            pltpu.VMEM((systems * DK, DK), F32),
            pltpu.VMEM((systems, DK, DK), F32),
            pltpu.VMEM((systems * EDGE // DK, DK, DK), F32),
            pltpu.VMEM((systems * EDGE, DK), F32),
            pltpu.VMEM((owners, rows, width), BF16),
            *[pltpu.VMEM((heads, DK, DK), F32)] * 6,
            dma((heads + 2, owners)), dma((heads + 2, owners)), dma((heads + 2,)),
            dma((owners,)), dma((owners,)), dma,
            *[dma((heads * DK // CHUNK,))] * 4,
        ],
        compiler_params=pltpu.CompilerParams(
            vmem_limit_bytes=67_000_000, collective_id=0, has_side_effects=True
        ),
    )(queries, key_rows, value_rows, ridge_diag)


def solution(mesh):
    in_specs = (P(("seq", "head"), None), P(("seq", "head"), None), P(("seq", "head"), None), P())
    out_specs = P(("seq", "head"), None)
    return jax.shard_map(body, mesh=mesh, in_specs=in_specs, out_specs=out_specs, check_vma=False)
```

```python
import functools

import jax
import jax.numpy as jnp
from jax import lax
from jax.experimental import pallas as pl
from jax.experimental.pallas import tpu as pltpu
from jax.sharding import PartitionSpec as P

DK = 128
GROUP = 64
EDGE = 32
BATCH = 16
SUBLANES = 8
CHUNK = 64
EPS = 1e-06
F32 = jnp.float32
BF16 = jnp.bfloat16


def unit(rows):
    wide = rows.astype(F32)
    back = lax.rsqrt(jnp.sum(wide * wide, axis=-1, keepdims=True) + EPS)
    return (wide * back).astype(BF16)


def split3(value):
    high = value.astype(BF16)
    rest = value - high.astype(F32)
    mid = rest.astype(BF16)
    low = (rest - mid.astype(F32)).astype(BF16)
    return high, mid, low


def dot(left, right, contract):
    return lax.dot_general(left, right, ((contract[:1], contract[1:]), ((), ())), preferred_element_type=F32)


def left_stack(parts):
    high, mid, low = parts
    return jnp.concatenate([high, high, mid, high, low, mid], axis=0)


def right_stack(parts):
    high, mid, low = parts
    return jnp.concatenate([high, mid, high, low, high, mid], axis=0)


def sweep_pair(tiles, turn, lane, sub):
    at, inner = turn // SUBLANES, turn % SUBLANES
    within = lane % SUBLANES
    pick1 = lane - within + inner
    pick2 = pick1 + 1
    first, second = within == inner, within == inner + 1
    either = jnp.logical_or(first, second)
    here1, here2 = sub == inner, sub == inner + 1
    here = jnp.logical_or(here1, here2)

    def take(block, pick):
        return jnp.take_along_axis(block, pick, axis=1, mode="promise_in_bounds")

    def spread(block, row):
        return jnp.broadcast_to(block[row : row + 1, :], block.shape)

    col1 = [take(block, pick1) for block in tiles[at]]
    col2 = [take(block, pick2) for block in tiles[at]]
    a, b, d = spread(col1[at], inner), spread(col2[at], inner), spread(col2[at], inner + 1)
    back = 1.0 / (a * d - b * b)
    e, f, h = d * back, b * back, a * back
    col1[at] = jnp.where(here1, -1.0, jnp.where(here2, 0.0, col1[at]))
    col2[at] = jnp.where(here2, -1.0, jnp.where(here1, 0.0, col2[at]))
    fresh = []
    for g, column in enumerate(tiles):
        row1, row2 = spread(column[at], inner), spread(column[at], inner + 1)
        if g == at:
            row1 = jnp.where(first, -1.0, jnp.where(second, 0.0, row1))
            row2 = jnp.where(second, -1.0, jnp.where(first, 0.0, row2))
        scaled1, scaled2 = e * row1 - f * row2, h * row2 - f * row1
        blocks = []
        for v, block in enumerate(column):
            if v == at:
                block = jnp.where(here, 0.0, block)
            if g == at:
                block = jnp.where(either, 0.0, block)
            blocks.append(block - (col1[v] * scaled1 + col2[v] * scaled2))
        fresh.append(blocks)
    return fresh


def invert_all(count, sys_ref, turn_ref, pinv_ref, midway):
    copies = DK // EDGE
    share = DK // SUBLANES
    bands = EDGE // SUBLANES
    lane = lax.broadcasted_iota(jnp.int32, (SUBLANES, DK), 1)
    sub = lax.broadcasted_iota(jnp.int32, (SUBLANES, DK), 0)
    lane32 = lax.broadcasted_iota(jnp.int32, (EDGE, DK), 1)
    sub32 = lax.broadcasted_iota(jnp.int32, (EDGE, DK), 0)
    row128 = lax.broadcasted_iota(jnp.int32, (DK, DK), 0) // EDGE
    lane128 = lax.broadcasted_iota(jnp.int32, (DK, DK), 1) // EDGE

    def panel(p, carry):
        @pl.when(p == copies // 2)
        def _():
            midway()

        start = pl.multiple_of(p * EDGE, EDGE)
        halves = []
        for half in range(count // share):
            tiles = []
            for g in range(bands):
                at = half * bands + g
                stacked = [
                    sys_ref[pl.ds(pl.multiple_of((half * share + s) * DK + start + g * SUBLANES, SUBLANES), SUBLANES), :]
                    for s in range(share)
                ]
                turn_ref[at] = jnp.transpose(jnp.concatenate(stacked, axis=0))
                tiles.append([
                    turn_ref[at, pl.ds(pl.multiple_of(start + v * SUBLANES, SUBLANES), SUBLANES), :] for v in range(bands)
                ])
            halves.append(tiles)
        for turn in range(0, EDGE, 2):
            halves = [sweep_pair(tiles, turn, lane, sub) for tiles in halves]
        for half, tiles in enumerate(halves):
            for g, column in enumerate(tiles):
                block = jnp.transpose(jnp.concatenate(column * copies, axis=0))
                for s in range(share):
                    row = (half * share + s) * EDGE + g * SUBLANES
                    pinv_ref[row : row + SUBLANES, :] = block[s * SUBLANES : (s + 1) * SUBLANES, :]

        mine = lane32 // EDGE == p
        diag = lane32 - p * EDGE == sub32
        cleared = jnp.logical_or(row128 == p, lane128 == p)
        third = lane32 // EDGE == 2
        first = lane32 // EDGE == 0

        def update(turn, carry):
            batch = [turn * BATCH + i for i in range(BATCH)]
            lefts, rows = [], []
            for g in batch:
                high, mid, low = split3(pinv_ref[pl.ds(pl.multiple_of(g * EDGE, EDGE), EDGE), :])
                left = jnp.concatenate([jnp.where(third, mid, high), jnp.where(first, low, mid)], axis=1)
                lefts.append(left[:, : 6 * EDGE])
                row = sys_ref[pl.ds(pl.multiple_of(g * DK, DK) + start, EDGE), :]
                rows.append(split3(jnp.where(mine, jnp.where(diag, -1.0, 0.0), row)))
            scaled = [dot(left, right_stack(r), (1, 0)) for left, r in zip(lefts, rows)]
            change = [dot(left_stack(r), right_stack(split3(t)), (0, 0)) for r, t in zip(rows, scaled)]
            for g, c in zip(batch, change):
                whole = pl.ds(pl.multiple_of(g * DK, DK), DK)
                sys_ref[whole, :] = jnp.where(cleared, 0.0, sys_ref[whole, :]) + c
            return carry

        return lax.fori_loop(0, count // BATCH, update, carry)

    lax.fori_loop(0, copies, panel, 0)


def whole_kernel(
    owners, shards, q_hbm, k_hbm, v_hbm, ridge_ref, out_hbm,
    q_all, k_all, v_all, sys_ref, vk_ref, turn_ref, pinv_ref, stage, gram_total, vk_total, gram_staged, vk_staged, gram_before, vk_before,
    send_sems, recv_sems, local_sems, out_send, out_recv, out_local, gram_send, gram_recv, vk_send, vk_recv,
):
    me, shard = lax.axis_index("head"), lax.axis_index("seq")
    rows_each = q_hbm.shape[0]
    width = q_all.shape[1]
    heads = width // DK
    per_source = rows_each // GROUP
    groups = owners * per_source
    moved = [(k_hbm, k_all, h * DK, DK) for h in range(heads)]
    moved += [(v_hbm, v_all, 0, width), (q_hbm, q_all, 0, width)]
    values, queries = heads, heads + 1

    def rows_of(source):
        return pl.ds(pl.multiple_of(source * rows_each, rows_each), rows_each)

    def cols_of(owner):
        return pl.ds(pl.multiple_of(owner * width, width), width)

    def source_part(kind, owner):
        ref, _, offset, size = moved[kind]
        return ref.at[:, pl.ds(pl.multiple_of(owner * width + offset, size), size)]

    def target_part(kind, source):
        _, ref, offset, size = moved[kind]
        return ref.at[rows_of(source), pl.ds(offset, size)]

    def incoming(kind, source):
        return pltpu.make_async_remote_copy(
            src_ref=source_part(kind, source),
            dst_ref=target_part(kind, source),
            send_sem=send_sems.at[kind, source],
            recv_sem=recv_sems.at[kind, source],
            device_id={"head": source},
            device_id_type=pl.DeviceIdType.MESH,
        )

    def outgoing(kind, peer):
        return pltpu.make_async_remote_copy(
            src_ref=source_part(kind, peer),
            dst_ref=target_part(kind, me),
            send_sem=send_sems.at[kind, peer],
            recv_sem=recv_sems.at[kind, me],
            device_id={"head": peer},
            device_id_type=pl.DeviceIdType.MESH,
        )

    def own(kind):
        return pltpu.make_async_copy(source_part(kind, me), target_part(kind, me), local_sems.at[kind])

    def chunk(c):
        return c * CHUNK // DK, pl.ds(c * CHUNK % DK, CHUNK)

    def link_copy(staged, before, send, recv, c, target):
        head, rows = chunk(c)
        return pltpu.make_async_remote_copy(
            src_ref=staged.at[head, rows, :],
            dst_ref=before.at[head, rows, :],
            send_sem=send.at[c],
            recv_sem=recv.at[c],
            device_id={"seq": target},
            device_id_type=pl.DeviceIdType.MESH,
        )

    chunks = heads * DK // CHUNK

    def pass_on(total, staged, before, send, recv, only=None):
        for c in range(chunks):
            head, rows = chunk(c)
            if only in (None, head):
                staged[head, rows, :] = total[head, rows, :] + before[head, rows, :]
                link_copy(staged, before, send, recv, c, shard + 1).start()

    def chain(total, staged, before, send, recv):
        for c in range(chunks):
            head, rows = chunk(c)
            link_copy(staged, before, send, recv, c, shard).wait_recv()

            @pl.when(shard + 1 < shards)
            def _():
                staged[head, rows, :] = total[head, rows, :] + before[head, rows, :]
                link_copy(staged, before, send, recv, c, shard + 1).start()

    def drain(staged, before, send, recv):
        for c in range(chunks):
            @pl.when(shard + 1 < shards)
            def _():
                link_copy(staged, before, send, recv, c, shard + 1).wait_send()

    barrier = pltpu.get_barrier_semaphore()
    for step in range(1, owners):
        pl.semaphore_signal(barrier, inc=1, device_id={"head": lax.rem(me + step, owners)}, device_id_type=pl.DeviceIdType.MESH)
    for near in (shard - 1, shard + 1):
        @pl.when(jnp.logical_and(near >= 0, near < shards))
        def _():
            pl.semaphore_signal(barrier, inc=1, device_id={"seq": near}, device_id_type=pl.DeviceIdType.MESH)
    for kind in range(len(moved)):
        own(kind).start()
    ends = (shard == 0).astype(jnp.int32) + (shard == shards - 1).astype(jnp.int32)
    pl.semaphore_wait(barrier, owners - 1 + 2 - ends)
    for kind in range(len(moved)):
        for step in range(1, owners):
            outgoing(kind, lax.rem(me + step, owners)).start()
    for kind in range(len(moved)):
        own(kind).wait()

    @pl.when(shard == 0)
    def _():
        gram_before[...] = jnp.zeros_like(gram_before)
        vk_before[...] = jnp.zeros_like(vk_before)

    def system(head, group):
        return pl.ds(pl.multiple_of((head * groups + group) * DK, DK), DK)

    def rows_in(source, i):
        return pl.ds(pl.multiple_of(source * rows_each + i * GROUP, GROUP), GROUP)

    def keys_of(h):
        cols = slice(h * DK, (h + 1) * DK)

        def keys_in(at, run):
            source = lax.rem(me + owners - at, owners)

            @pl.when(source != me)
            def _():
                incoming(h, source).wait_recv()

            adds = []
            for i in range(per_source):
                ku = unit(k_all[rows_in(source, i), cols])
                k_all[rows_in(source, i), cols] = ku
                adds.append(dot(ku, ku, (0, 0)))
            for i in range(per_source):
                sys_ref[system(h, source * per_source + i), :] = adds[i]
                run = run + adds[i]
            return run

        gram_total[h] = lax.fori_loop(0, owners, keys_in, jnp.zeros((DK, DK), F32))

    zero = tuple(jnp.zeros((DK, DK), F32) for _ in range(heads))
    for h in range(heads):
        keys_of(h)

        @pl.when(jnp.logical_and(shard == 0, shard + 1 < shards))
        def _():
            pass_on(gram_total, gram_staged, gram_before, gram_send, gram_recv, h)

    @pl.when(shard > 0)
    def _():
        chain(gram_total, gram_staged, gram_before, gram_send, gram_recv)


    def values_in(source, runs):
        @pl.when(source != me)
        def _():
            incoming(values, source).wait_recv()

        adds = []
        for h in range(heads):
            for i in range(per_source):
                cols = slice(h * DK, (h + 1) * DK)
                adds.append(dot(k_all[rows_in(source, i), cols], v_all[rows_in(source, i), cols], (0, 0)))
        runs = list(runs)
        for h in range(heads):
            for i in range(per_source):
                vk_ref[h * groups + source * per_source + i] = runs[h]
                runs[h] = runs[h] + adds[h * per_source + i]
        return tuple(runs)

    def values_out():
        runs = lax.fori_loop(0, owners, values_in, zero)
        for h in range(heads):
            vk_total[h] = runs[h]

        @pl.when(jnp.logical_and(shard == 0, shard + 1 < shards))
        def _():
            pass_on(vk_total, vk_staged, vk_before, vk_send, vk_recv)

        @pl.when(shard > 0)
        def _():
            chain(vk_total, vk_staged, vk_before, vk_send, vk_recv)

    eye = lax.broadcasted_iota(jnp.int32, (DK, DK), 0) == lax.broadcasted_iota(jnp.int32, (DK, DK), 1)

    def start_of(c, runs):
        runs = list(runs)
        for h in range(heads):
            own_gram = sys_ref[system(h, c), :]
            sys_ref[system(h, c), :] = runs[h]
            runs[h] = runs[h] + own_gram
        return tuple(runs)

    lax.fori_loop(
        0, groups, start_of,
        tuple(gram_before[h] + jnp.where(eye, ridge_ref[pl.ds(me * heads + h, 1), :], 0.0) for h in range(heads)),
    )

    invert_all(heads * groups, sys_ref, turn_ref, pinv_ref, values_out)

    for step in range(1, owners):
        incoming(queries, lax.rem(me + step, owners)).wait_recv()

    def result_copy(peer):
        return pltpu.make_async_remote_copy(
            src_ref=stage.at[peer],
            dst_ref=out_hbm.at[:, cols_of(me)],
            send_sem=out_send.at[peer],
            recv_sem=out_recv.at[me],
            device_id={"head": peer},
            device_id_type=pl.DeviceIdType.MESH,
        )

    sub = lax.broadcasted_iota(jnp.int32, (GROUP, 2 * GROUP), 0)
    lane = lax.broadcasted_iota(jnp.int32, (GROUP, 2 * GROUP), 1)
    twice = lane >= GROUP
    causal = jnp.where(twice, lane - GROUP, lane) <= sub

    def finish(step, carry):
        source = lax.rem(me + 1 + step, owners)
        jobs = [(h, i) for h in range(heads) for i in range(per_source)]
        solved = []
        for h, i in jobs:
            qu = unit(q_all[rows_in(source, i), h * DK : (h + 1) * DK])
            full = jnp.concatenate(split3(sys_ref[system(h, source * per_source + i), :]), axis=0)
            solved.append(split3(-dot(jnp.concatenate([qu, qu, qu], axis=1), full, (1, 0))))
        scores, carried = [], []
        for (h, i), (high, mid, low) in zip(jobs, solved):
            ku = k_all[rows_in(source, i), h * DK : (h + 1) * DK]
            ku = jnp.concatenate([ku, ku], axis=0)
            ku = jnp.concatenate([ku, ku, ku], axis=1)
            scores.append(dot(jnp.concatenate([high, mid, low], axis=1), ku, (1, 1)))
            left = jnp.concatenate([high, high, mid, high, low, mid], axis=1)
            start = vk_ref[h * groups + source * per_source + i] + vk_before[h]
            carried.append(dot(left, right_stack(split3(start)), (1, 0)))
        for (h, i), score, carry_in in zip(jobs, scores, carried):
            score = jnp.where(causal, score, 0.0)
            high = score.astype(BF16).astype(F32)
            both = jnp.where(twice, score - high, high).astype(BF16)
            vb = v_all[rows_in(source, i), h * DK : (h + 1) * DK]
            inner = dot(both, jnp.concatenate([vb, vb], axis=0), (1, 0))
            stage[source, i * GROUP : (i + 1) * GROUP, h * DK : (h + 1) * DK] = (carry_in + inner).astype(BF16)

        @pl.when(source != me)
        def _():
            result_copy(source).start()

        return carry

    lax.fori_loop(0, owners, finish, 0)
    mine = pltpu.make_async_copy(stage.at[me], out_hbm.at[:, cols_of(me)], out_local)
    mine.start()
    for step in range(1, owners):
        peer = lax.rem(me + step, owners)
        for kind in range(len(moved)):
            outgoing(kind, peer).wait_send()
        result_copy(peer).wait_send()
    for step in range(1, owners):
        source = lax.rem(me + step, owners)
        pltpu.make_async_remote_copy(
            src_ref=stage.at[source],
            dst_ref=out_hbm.at[:, cols_of(source)],
            send_sem=out_send.at[source],
            recv_sem=out_recv.at[source],
            device_id={"head": source},
            device_id_type=pl.DeviceIdType.MESH,
        ).wait_recv()
    mine.wait()
    drain(gram_staged, gram_before, gram_send, gram_recv)
    drain(vk_staged, vk_before, vk_send, vk_recv)


def body(queries, key_rows, value_rows, ridge_diag):
    owners, shards = lax.axis_size("head"), lax.axis_size("seq")
    rows, columns = queries.shape
    width = columns // owners
    heads = width // DK
    tokens = rows * owners
    systems = heads * (tokens // GROUP)
    anywhere = pl.BlockSpec(memory_space=pltpu.HBM)
    dma = pltpu.SemaphoreType.DMA
    return pl.pallas_call(
        functools.partial(whole_kernel, owners, shards),
        out_shape=jax.ShapeDtypeStruct((rows, columns), BF16),
        in_specs=[anywhere] * 3 + [pl.BlockSpec(memory_space=pltpu.VMEM)],
        out_specs=anywhere,
        scratch_shapes=[
            pltpu.VMEM((tokens, width), BF16),
            pltpu.VMEM((tokens, width), BF16),
            pltpu.VMEM((tokens, width), BF16),
            pltpu.VMEM((systems * DK, DK), F32),
            pltpu.VMEM((systems, DK, DK), F32),
            pltpu.VMEM((systems * EDGE // DK, DK, DK), F32),
            pltpu.VMEM((systems * EDGE, DK), F32),
            pltpu.VMEM((owners, rows, width), BF16),
            *[pltpu.VMEM((heads, DK, DK), F32)] * 6,
            dma((heads + 2, owners)), dma((heads + 2, owners)), dma((heads + 2,)),
            dma((owners,)), dma((owners,)), dma,
            *[dma((heads * DK // CHUNK,))] * 4,
        ],
        compiler_params=pltpu.CompilerParams(
            vmem_limit_bytes=67_000_000, collective_id=0, has_side_effects=True
        ),
    )(queries, key_rows, value_rows, ridge_diag)


def solution(mesh):
    in_specs = (P(("seq", "head"), None), P(("seq", "head"), None), P(("seq", "head"), None), P())
    out_specs = P(("seq", "head"), None)
    return jax.shard_map(body, mesh=mesh, in_specs=in_specs, out_specs=out_specs, check_vma=False)
```
